512 devices in a mesh: dp: 4 (over x), expert: 64 (over z, y), tensor: 2 (over core).
Axes of the slice: x: 4, y: 8, z: 8, core: 2. Of those that a mesh axis runs over, the one named last changes fastest.
Arguments:
- out_grad: bfloat16 [32768, 3584], P(('dp', 'expert'), 'tensor'), may hold values from -6 to 6
- routing: int32 [32768, 8], P(('dp', 'expert')), may hold values from 0 to 255, all different within a row; in each aligned block of 128 rows (0 to 127, 128 to 255, ...) at most 8 rows name the same one
- route_probs: float32 [32768, 8], P(('dp', 'expert')), may hold values from 0.05 to 1
- w_down: bfloat16 [64, 3584, 1024], P('expert', 'dp', 'tensor'), may hold values from -0.1875 to 0.1875
- saved_gate: bfloat16 [131072, 1024], P(('dp', 'expert'), 'tensor'), may hold values from -8 to 8
- saved_up: bfloat16 [131072, 1024], P(('dp', 'expert'), 'tensor'), may hold values from -6 to 6
Outputs:
- weight_grad: bfloat16 [64, 3584, 1024], P('expert', 'dp', 'tensor')
- grad_gate: bfloat16 [131072, 1024], P(('dp', 'expert'), 'tensor')
- grad_up: bfloat16 [131072, 1024], P(('dp', 'expert'), 'tensor')
- grad_amax: float32 [4, 64], P('dp', 'expert')
The draws below stay inside these ranges and needn't reach their ends.
Inputs may be any that keep to these rules, and one draw needn't show every extreme that they name: `routing`: each row names 8 different experts; in the rows of one device no expert is named more than 8 times.
All inputs are finite; a program needn't handle non-finite values. Where the reference program divides by a largest or mean magnitude, that divisor is 1e-20 or more.
Results may differ from the reference program's by a relative error of at most 0.009.
Values may be sent and summed in bfloat16 or wider, within the bound.
A program may use at most 64 MiB of HBM per device.

```python
import math
import jax
import jax.numpy as jnp
import numpy as np
from jax import lax

D = 3584
F = 1024
TOP = 8
TOK_DEV = 128
EXPERTS = 256
CAP = 8
SLOTS = 512
TOKENS = 32768
N_DP = 4
N_EXPERT = 64


def block_scale(key, dims, shards, smallest, largest):
    level = 1.0
    for axis_at, blocks in shards:
        heights = jax.random.uniform(jax.random.fold_in(jax.random.fold_in(key, 6), axis_at), (blocks,), jnp.float32, smallest / len(shards), largest / len(shards))
        level = level * jnp.repeat(jnp.exp(heights), dims[axis_at] // blocks).reshape((-1,) + (1,) * (len(dims) - 1 - axis_at))
    return level


def routed_block(own_key, own, number, rows, count, top, most, skew):
    ranking = jax.random.permutation(own_key, count)
    heavy_load, usual = portions_of(count, rows * top, most, skew, True), portions_of(count, rows * top, most, skew, False)
    places = jnp.arange(count)

    def named(lengths, offset_by):
        used = int((lengths > 0).sum())
        fixed = max(1, used // 4)
        moved = fixed + (places - fixed + offset_by * (used - fixed)) % max(1, count - fixed)
        return jnp.zeros((count,), jnp.int32).at[ranking[jnp.where(places < fixed, places, moved)]].set(jnp.asarray(lengths, jnp.int32))

    lengths = jnp.where(number % 4 == 0, named(heavy_load, number // 4), named(usual, number - number // 4 - 1))
    mixed = jax.random.permutation(jax.random.fold_in(own, 3), count)
    donor, receiver = mixed[0:count // 2 * 2:2], mixed[1:count // 2 * 2:2]
    slack = jnp.minimum(lengths[donor] - 1, most - lengths[receiver]) // 2
    slack = jnp.where((donor == ranking[0]) | (receiver == ranking[0]) | (lengths[receiver] == 0), 0, jnp.maximum(slack, 0))
    moved = jax.random.randint(jax.random.fold_in(own, 4), (count // 2,), 0, 1 << 20) % (slack + 1)
    lengths = lengths.at[donor].add(-moved).at[receiver].add(moved)
    items = jnp.searchsorted(jnp.cumsum(lengths), jnp.arange(rows * top), side="right").astype(jnp.int32)
    table = items.reshape(top, rows).T
    table = table[jax.random.permutation(jax.random.fold_in(own, 1), rows)]
    offset_by = jax.random.randint(jax.random.fold_in(own, 2), (rows, 1), 0, top)
    return jnp.take_along_axis(table, (jnp.arange(top)[None, :] + offset_by) % top, axis=1)


def portions_of(amount, total, limit, lean, full):
    loads = [(1 << 20) // math.isqrt(rank ** lean) + 1 for rank in range(1, amount + 1)]
    largest = limit if full else min(limit, max(-(-total // amount), total * loads[0] // sum(loads)))
    least = 1 if total - largest >= amount - 1 else 0
    given, surplus = [largest] + [least] * (amount - 1), total - largest - least * (amount - 1)
    while surplus > 0:
        candidates = [i for i in range(1, amount) if given[i] < largest] or [i for i in range(1, amount) if given[i] < limit]
        pool, budget = sum([loads[i] for i in candidates]), surplus
        for i in candidates:
            more = min(limit - given[i], max(1, budget * loads[i] // pool), surplus)
            given[i] = given[i] + more
            surplus = surplus - more
    return np.array(given)


def gaussian(own_key, dims, spread, reach, cuts=(), kind=jnp.bfloat16):
    entries = jax.random.normal(own_key, dims, jnp.float32) * spread
    if len(cuts) > 0:
        entries = block_scale(own_key, dims, cuts, -0.22, 0.18) * entries
    return jnp.clip(entries, min=-reach, max=reach).astype(kind)


def setup_inputs(seed: int = 0) -> dict:
    splits = jax.random.split(jax.random.key(seed), 7)
    out_grad = gaussian(splits[0], (TOKENS, D), 1.0, 6.0, ((0, 256), (1, 2)))
    routing_keys = jax.random.split(jax.random.fold_in(splits[1], 1), TOKENS // TOK_DEV)
    routing_turns = jax.random.permutation(jax.random.fold_in(splits[1], 3), TOKENS // TOK_DEV)
    routing = jax.vmap(lambda own, number: routed_block(jax.random.fold_in(splits[1], 2), own, number, TOK_DEV, EXPERTS, TOP, CAP, 2))(routing_keys, routing_turns).reshape((TOKENS, TOP))
    route_probs = jnp.clip(jnp.exp(math.log(1.0) - 2.9957323 * jax.random.uniform(splits[2], (TOKENS, TOP), jnp.float32) ** block_scale(splits[2], (TOKENS, TOP), ((0, 256),), -0.2, 0.2)), 0.05, 1.0)
    w_down = gaussian(splits[3], (N_EXPERT, D, F), F ** -0.5, 0.1875, ((0, 64), (1, 4), (2, 2)))
    saved_gate = gaussian(splits[4], (N_DP * N_EXPERT * SLOTS, F), 2.0, 8.0, ((0, 256), (1, 2)))
    saved_up = gaussian(splits[5], (N_DP * N_EXPERT * SLOTS, F), 1.0, 6.0, ((0, 256), (1, 2)))
    return {"out_grad": out_grad, "routing": routing, "route_probs": route_probs, "w_down": w_down, "saved_gate": saved_gate, "saved_up": saved_up}


epsilon = 1e-6


def reference(out_grad, routing, route_probs, w_down, saved_gate, saved_up):
    owners = N_EXPERT
    blocks = N_DP * N_EXPERT
    slot_count = N_EXPERT * CAP
    total = N_DP * N_EXPERT * slot_count
    matches = routing[:, :, None] == jnp.arange(owners, dtype=jnp.int32)[None, None, :]
    is_routed = jnp.any(matches, axis=1).astype(jnp.int32)
    scaling = jnp.sum(jnp.where(matches, route_probs[:, :, None], 0.0), axis=1)
    per_block = is_routed.reshape(blocks, TOK_DEV, owners)
    slot_rank = jnp.cumsum(per_block, axis=1) - per_block
    block_ids = jnp.arange(blocks, dtype=jnp.int32)[:, None, None]
    group_ids = block_ids // owners
    source_ids = block_ids % owners
    expert_ids = jnp.arange(owners, dtype=jnp.int32)[None, None, :]
    target = ((group_ids * owners + expert_ids) * owners + source_ids) * CAP + slot_rank
    target = jnp.where(per_block == 1, target, total).reshape(-1).astype(jnp.int32)
    token_ids = jnp.broadcast_to(jnp.arange(blocks * TOK_DEV, dtype=jnp.int32).reshape(blocks, TOK_DEV, 1), per_block.shape).reshape(-1)
    slot_token = jnp.zeros((total,), jnp.int32).at[target].set(token_ids, mode="drop")
    slot_scale = jnp.zeros((total,), scaling.dtype).at[target].set(scaling.reshape(-1), mode="drop")

    def per_expert(expert_id):
        weight = lax.dynamic_index_in_dim(w_down, expert_id, 0, keepdims=False)
        summed = jnp.zeros((D, F), jnp.float32)
        gates = []
        ups = []
        maxima = []
        for group_id in range(N_DP):
            start = ((group_id * owners + expert_id) * slot_count).astype(jnp.int32)
            tokens = lax.dynamic_slice_in_dim(slot_token, start, slot_count)
            scales = lax.dynamic_slice_in_dim(slot_scale, start, slot_count)
            slot_rows = (jnp.take(out_grad, tokens, axis=0).astype(jnp.float32) * scales[:, None]).astype(jnp.bfloat16)
            grad_hidden = jnp.dot(slot_rows, weight, preferred_element_type=jnp.float32)
            grad_amax = jnp.max(jnp.abs(grad_hidden))
            quantized = lax.optimization_barrier((grad_hidden / (grad_amax + epsilon)).astype(jnp.bfloat16)).astype(jnp.float32)
            gate_pre = lax.dynamic_slice_in_dim(saved_gate, start, slot_count).astype(jnp.float32)
            up_pre = lax.dynamic_slice_in_dim(saved_up, start, slot_count).astype(jnp.float32)
            sigmoid_gate = jax.nn.sigmoid(gate_pre)
            silu_gate = gate_pre * sigmoid_gate
            gates.append((quantized * up_pre * sigmoid_gate * (1.0 + gate_pre * (1.0 - sigmoid_gate))).astype(jnp.bfloat16))
            ups.append((quantized * silu_gate).astype(jnp.bfloat16))
            activation = (silu_gate * up_pre).astype(jnp.bfloat16)
            partial_value = lax.dot_general(slot_rows, activation, (((0,), (0,)), ((), ())), preferred_element_type=jnp.float32)
            summed = summed + lax.optimization_barrier(partial_value.astype(jnp.bfloat16)).astype(jnp.float32)
            maxima.append(grad_amax)
        return summed.astype(jnp.bfloat16), jnp.stack(gates), jnp.stack(ups), jnp.stack(maxima)

    grads, gates, ups, maxima = lax.map(per_expert, jnp.arange(owners, dtype=jnp.int32))
    grad_gate = jnp.transpose(gates, (1, 0, 2, 3)).reshape(total, F)
    grad_up = jnp.transpose(ups, (1, 0, 2, 3)).reshape(total, F)
    return grads, grad_gate, grad_up, jnp.transpose(maxima)
```

```python
import functools
import math

import jax
import jax.numpy as jnp
from jax import lax
from jax.experimental import pallas as pl
from jax.experimental.pallas import tpu as pltpu
from jax.sharding import PartitionSpec as P

MESH = pl.DeviceIdType.MESH
EPSILON = 1e-6
F32 = jnp.float32
BF16 = jnp.bfloat16


def kernel(
    nz, ny, og, ids, probs, w, gate, up,
    wg_out, gg_out, gu_out, amax_out,
    gv, uv, wv, a1, a2, tok, idb, prb, keyb, scb, S, X, act,
    gh, wacc, far_out, far_in, near_out, near_in, mx_out, mx_in,
    loc_sem, id_send, id_recv, pr_send, pr_recv, tok_send, tok_recv, tokf_send,
    act_send, act_recv, actf_send, actf_recv,
    a2a_send, a2a_recv, fwd_send, fwd_recv,
    far_send, far_recv, near_send, near_recv, mx_send, mx_recv,
):
    q = lax.axis_index("dp")
    e = lax.axis_index("expert")
    t = lax.axis_index("tensor")
    z = e // ny
    y = lax.rem(e, ny)
    half = nz // 2
    ne = nz * ny
    tokens, dc = tok.shape[1], tok.shape[2]
    top = ids.shape[0]
    cap = S.shape[3]
    slots, fh = gate.shape
    sh = slots // 2
    right, opposite, left = lax.rem(q + 1, 4), lax.rem(q + 2, 4), lax.rem(q + 3, 4)
    partner = (q, e, 1 - t)

    def rcopy(src, dst, ss, rs, dev):
        return pltpu.make_async_remote_copy(
            src_ref=src, dst_ref=dst, send_sem=ss, recv_sem=rs, device_id=dev, device_id_type=MESH
        )

    copy_g = pltpu.make_async_copy(gate, gv, loc_sem.at[0])
    copy_u = pltpu.make_async_copy(up, uv, loc_sem.at[1])
    copy_w = pltpu.make_async_copy(w, wv, loc_sem.at[2])
    copy_g.start()
    copy_u.start()
    copy_w.start()

    barrier = pltpu.get_barrier_semaphore()
    for r in range(1, 4):
        pl.semaphore_signal(barrier, inc=1, device_id=(lax.rem(q + r, 4), e, t), device_id_type=MESH)
    pl.semaphore_signal(barrier, inc=1, device_id=partner, device_id_type=MESH)

    def greet(n, carry):
        dz, dy = 2 * (n // ny) + t, lax.rem(n, ny)
        peer = lax.rem(z + dz, nz) * ny + lax.rem(y + dy, ny)

        @pl.when(dz + dy > 0)
        def _():
            pl.semaphore_signal(barrier, inc=1, device_id=(q, peer, t), device_id_type=MESH)

        return carry

    lax.fori_loop(0, half * ny, greet, 0)

    copy_g.wait()
    copy_u.wait()
    rows = slots // nz

    def activate(n, carry):
        at = pl.ds(pl.multiple_of(n * rows, rows), rows)
        g = gv[at, :].astype(F32)
        u = uv[at, :].astype(F32)
        s = jax.nn.sigmoid(g)
        silu = g * s
        act[0, at, :] = (silu * u).astype(BF16)
        a1[at, :] = u * s * (1.0 + g * (1.0 - s))
        a2[at, :] = silu
        return carry

    lax.fori_loop(0, nz, activate, 0)

    def make_key(r, id_rows, pr_rows):
        owner = lax.broadcasted_iota(jnp.int32, (ne, tokens), 0)
        routed = jnp.zeros((ne, tokens), F32)
        scale = jnp.zeros((ne, tokens), F32)
        for k in range(top):
            match = owner == id_rows[k : k + 1, :]
            routed = jnp.where(match, 1.0, routed)
            scale = scale + jnp.where(match, pr_rows[k : k + 1, :], 0.0)
        before = lax.broadcasted_iota(jnp.int32, (tokens, tokens), 0)
        after = lax.broadcasted_iota(jnp.int32, (tokens, tokens), 1)
        upper = jnp.where(before < after, 1.0, 0.0).astype(BF16)
        rank = jnp.dot(routed.astype(BF16), upper, preferred_element_type=F32)
        keyb[r] = jnp.where(routed > 0.0, rank, -1.0)
        scb[r] = scale

    make_key(0, ids[...], probs[...])

    pl.semaphore_wait(barrier, half * ny + 3 + t)

    for j in range(2):
        dest = 2 * t + j
        source = og.at[:, pl.ds(j * dc, dc)]

        @pl.when(dest != q)
        def _():
            slot = lax.rem(q - dest + 4, 4)
            rcopy(source, tok.at[slot], tok_send.at[j], tok_recv.at[slot], (dest, e, t)).start()

        @pl.when(dest == q)
        def _():
            pltpu.make_async_copy(source, tok.at[0], tok_recv.at[0]).start()
            rcopy(source, tok.at[0], tokf_send.at[0], tok_recv.at[0], partner).start()

    for r in (2, 1, 3):
        peer = (lax.rem(q + r, 4), e, t)
        slot = (4 - r) % 4
        rcopy(ids, idb.at[slot], id_send.at[r], id_recv.at[slot], peer).start()
        rcopy(probs, prb.at[slot], pr_send.at[r], pr_recv.at[slot], peer).start()
    rcopy(act.at[0], act.at[3], act_send.at[0], act_recv.at[0], (right, e, t)).start()
    rcopy(act.at[0], act.at[1], act_send.at[1], act_recv.at[1], (left, e, t)).start()

    holder = lax.div(q, 2) == t

    def get_tokens(r):
        rcopy(tok.at[r], tok.at[r], tokf_send.at[r], tok_recv.at[r], partner).wait_recv()
        if r > 0:

            @pl.when(holder)
            def _():
                rcopy(tok.at[r], tok.at[r], tokf_send.at[r], tok_recv.at[r], partner).start()

            rcopy(ids, idb.at[r], id_send.at[r], id_recv.at[r], partner).wait_recv()
            rcopy(probs, prb.at[r], pr_send.at[r], pr_recv.at[r], partner).wait_recv()
            make_key(r, idb[r], prb[r])

    rank_of = lax.broadcasted_iota(jnp.int32, (cap, tokens), 0).astype(F32)

    def send_rows(r, first, last):
        def build(i):
            zz = lax.rem(z + 2 * i + t, nz)
            at = pl.ds(pl.multiple_of(zz * ny, ny), ny)
            keys, scales = keyb[r, at, :], scb[r, at, :]
            picks, weights = [], []
            for yy in range(ny):
                hit = keys[yy : yy + 1, :] == rank_of
                picks.append(jnp.where(hit, 1.0, 0.0))
                weights.append(jnp.sum(jnp.where(hit, scales[yy : yy + 1, :], 0.0), axis=1, keepdims=True))
            pick = jnp.concatenate(picks, axis=0).astype(BF16)
            weight = jnp.concatenate(weights, axis=0)
            value = jnp.dot(pick, tok[r], preferred_element_type=F32) * weight
            for yy in range(ny):
                S[r, zz, yy] = value[yy * cap : (yy + 1) * cap, :].astype(BF16)

        def send(i):
            dz = 2 * i + t
            zz = lax.rem(z + dz, nz)

            def one(dy, carry):
                yy = lax.rem(y + dy, ny)

                @pl.when(dz + dy > 0)
                def _():
                    rcopy(
                        S.at[r, zz, yy], X.at[r, z, y], a2a_send.at[r, i], a2a_recv.at[r, i], (q, zz * ny + yy, t)
                    ).start()

                @pl.when(dz + dy == 0)
                def _():
                    pltpu.make_async_copy(S.at[r, zz, yy], X.at[r, z, y], a2a_recv.at[r, i]).start()

                return carry

            lax.fori_loop(0, ny, one, 0)

        build(first)

        def step(i, carry):
            build(i)
            send(i - 1)
            return carry

        lax.fori_loop(first + 1, last, step, 0)
        return lambda: send(last - 1)

    split = max(1, half // 2)
    get_tokens(0)
    finish = send_rows(0, 0, split)
    get_tokens(2)
    finish()
    finish = send_rows(2, 0, half)
    get_tokens(1)
    finish()
    finish = send_rows(1, 0, half)
    get_tokens(3)
    finish()
    finish = send_rows(3, 0, half)
    rcopy(act.at[0], act.at[3], act_send.at[0], act_recv.at[0], (right, e, t)).wait_recv()
    low, high = pl.ds(0, sh), pl.ds(sh, sh)
    rcopy(act.at[3, low], act.at[2, low], actf_send.at[0], actf_recv.at[0], (right, e, t)).start()
    rcopy(act.at[0], act.at[1], act_send.at[1], act_recv.at[1], (left, e, t)).wait_recv()
    rcopy(act.at[1, high], act.at[2, high], actf_send.at[1], actf_recv.at[1], (left, e, t)).start()
    finish()
    if split < half:
        finish = send_rows(0, split, half)
    else:
        finish = lambda: None

    def arrive(r, first, last):
        def step(i, carry):
            zs = lax.rem(z - (2 * i + t) + nz, nz)
            block = X.at[r, zs]
            rcopy(block, block, fwd_send.at[r, i], a2a_recv.at[r, i], partner).wait_recv()
            rcopy(block, block, fwd_send.at[r, i], fwd_recv.at[r, i], partner).start()
            return carry

        lax.fori_loop(first, last, step, 0)

    def arrive_partner(r):
        def step(i, carry):
            zs = lax.rem(z - (2 * i + 1 - t) + nz, nz)
            block = X.at[r, zs]
            rcopy(block, block, fwd_send.at[r, i], fwd_recv.at[r, i], partner).wait_recv()
            return carry

        lax.fori_loop(0, half, step, 0)

    def grad_hidden(r):
        for h in range(2):
            block = X[r, h * half : (h + 1) * half].reshape(sh, dc)
            gh[h * sh : (h + 1) * sh, :] = jnp.dot(block, wv[...], preferred_element_type=F32)

    def weight_grad(r, init):
        step = 128

        def body(n, carry):
            at = pl.ds(pl.multiple_of(n * step, step), step)
            block = X[r, :, :, :, at].reshape(slots, step)
            value = lax.dot_general(block, act[r], (((0,), (0,)), ((), ())), preferred_element_type=F32)
            if init:
                wacc[at, :] = value
            else:
                wacc[at, :] += value
            return carry

        lax.fori_loop(0, dc // step, body, 0)

    arrive(0, 0, split)
    finish()
    copy_w.wait()

    arrive(2, 0, half)
    arrive_partner(2)
    grad_hidden(2)
    far_out[...] = gh[...].astype(BF16)
    rcopy(act.at[3, low], act.at[2, low], actf_send.at[0], actf_recv.at[0], (right, e, t)).wait_recv()
    rcopy(act.at[1, high], act.at[2, high], actf_send.at[1], actf_recv.at[1], (left, e, t)).wait_recv()
    rcopy(far_out.at[low], far_in.at[0], far_send.at[0], far_recv.at[0], (right, e, t)).start()
    rcopy(far_out.at[high], far_in.at[1], far_send.at[1], far_recv.at[1], (left, e, t)).start()
    weight_grad(2, True)

    for n, (r, dest, part) in enumerate(((1, right, low), (3, left, high))):
        arrive(r, 0, half)
        arrive_partner(r)
        grad_hidden(r)
        rcopy(far_out.at[part], far_in.at[n], far_send.at[n], far_recv.at[n], (dest, e, t)).wait_recv()
        gh[part, :] += far_in[n].astype(F32)
        near_out[n] = gh[...].astype(BF16)
        weight_grad(r, False)
        rcopy(near_out.at[n], near_in.at[n], near_send.at[n], near_recv.at[n], (dest, e, t)).start()

    arrive(0, split, half)
    arrive_partner(0)
    grad_hidden(0)
    for n, dest in ((0, right), (1, left)):
        rcopy(near_out.at[n], near_in.at[n], near_send.at[n], near_recv.at[n], (dest, e, t)).wait_recv()

    def total(n, largest):
        at = pl.ds(pl.multiple_of(n * rows, rows), rows)
        value = gh[at, :] + near_in[0, at, :].astype(F32) + near_in[1, at, :].astype(F32)
        gh[at, :] = value
        return jnp.maximum(largest, jnp.max(jnp.abs(value)))

    largest = lax.fori_loop(0, nz, total, jnp.zeros((), F32))
    mx_out[...] = jnp.full(mx_out.shape, largest, F32)
    weight_grad(0, False)
    exchange = rcopy(mx_out, mx_in, mx_send.at[0], mx_recv.at[0], partner)
    exchange.start()
    wg_out[...] = wacc[...].astype(BF16)
    exchange.wait_recv()
    amax = jnp.maximum(mx_out[...], mx_in[...])
    amax_out[...] = amax
    inverse = 1.0 / (amax[0:1, 0:1] + EPSILON)

    def scale_out(n, carry):
        at = pl.ds(pl.multiple_of(n * rows, rows), rows)
        quantized = (gh[at, :] * inverse).astype(BF16).astype(F32)
        gg_out[at, :] = (quantized * a1[at, :]).astype(BF16)
        gu_out[at, :] = (quantized * a2[at, :]).astype(BF16)
        return carry

    lax.fori_loop(0, nz, scale_out, 0)

    for j in range(2):
        source = og.at[:, pl.ds(j * dc, dc)]

        @pl.when(2 * t + j != q)
        def _():
            rcopy(source, tok.at[0], tok_send.at[j], tok_recv.at[0], partner).wait_send()

        @pl.when(2 * t + j == q)
        def _():
            rcopy(source, tok.at[0], tokf_send.at[0], tok_recv.at[0], partner).wait_send()

    for r in range(1, 4):

        @pl.when(holder)
        def _():
            rcopy(tok.at[r], tok.at[r], tokf_send.at[r], tok_recv.at[r], partner).wait_send()

        rcopy(ids, idb.at[r], id_send.at[r], id_recv.at[r], partner).wait_send()
        rcopy(probs, prb.at[r], pr_send.at[r], pr_recv.at[r], partner).wait_send()
    for n in range(2):
        rcopy(act.at[0], act.at[1], act_send.at[n], act_recv.at[n], partner).wait_send()
        rcopy(act.at[1, low], act.at[2, low], actf_send.at[n], actf_recv.at[n], partner).wait_send()
        rcopy(far_out.at[low], far_in.at[n], far_send.at[n], far_recv.at[n], partner).wait_send()
        rcopy(near_out.at[n], near_in.at[n], near_send.at[n], near_recv.at[n], partner).wait_send()
    exchange.wait_send()
    for r in range(4):

        def drain(i, carry):
            block = X.at[r, 0]
            rcopy(block, block, fwd_send.at[r, i], fwd_recv.at[r, i], partner).wait_send()

            @pl.when(i + t > 0)
            def _():
                rcopy(S.at[r, 0], block, a2a_send.at[r, i], a2a_recv.at[r, i], partner).wait_send()

            @pl.when(i + t == 0)
            def _():
                some = pl.ds(0, ny - 1)
                rcopy(
                    S.at[r, 0, some], X.at[r, 0, some], a2a_send.at[r, i], a2a_recv.at[r, i], partner
                ).wait_send()

            return carry

        lax.fori_loop(0, half, drain, 0)


def body(side, out_grad, routing, route_probs, w_down, saved_gate, saved_up):
    nz = ny = side
    tokens, wide = out_grad.shape
    _, dc, fh = w_down.shape
    slots = saved_gate.shape[0]
    cap = slots // (nz * ny)
    top = routing.shape[1]
    half = nz // 2
    dma = pltpu.SemaphoreType.DMA
    scratch = [
        pltpu.VMEM((slots, fh), BF16),
        pltpu.VMEM((slots, fh), BF16),
        pltpu.VMEM((dc, fh), BF16),
        pltpu.VMEM((slots, fh), F32),
        pltpu.VMEM((slots, fh), F32),
        pltpu.VMEM((4, tokens, dc), BF16),
        pltpu.VMEM((4, top, tokens), jnp.int32),
        pltpu.VMEM((4, top, tokens), F32),
        pltpu.VMEM((4, nz * ny, tokens), F32),
        pltpu.VMEM((4, nz * ny, tokens), F32),
        pltpu.VMEM((4, nz, ny, cap, dc), BF16),
        pltpu.VMEM((4, nz, ny, cap, dc), BF16),
        pltpu.VMEM((4, slots, fh), BF16),
        pltpu.VMEM((slots, fh), F32),
        pltpu.VMEM((dc, fh), F32),
        pltpu.VMEM((slots, fh), BF16),
        pltpu.VMEM((2, slots // 2, fh), BF16),
        pltpu.VMEM((2, slots, fh), BF16),
        pltpu.VMEM((2, slots, fh), BF16),
        pltpu.VMEM((8, 128), F32),
        pltpu.VMEM((8, 128), F32),
        dma((3,)),
        dma((4,)), dma((4,)), dma((4,)), dma((4,)),
        dma((2,)), dma((4,)), dma((4,)),
        dma((2,)), dma((2,)), dma((2,)), dma((2,)),
        dma((4, half)), dma((4, half)), dma((4, half)), dma((4, half)),
        dma((2,)), dma((2,)), dma((2,)), dma((2,)), dma((1,)), dma((1,)),
    ]
    vmem = pl.BlockSpec(memory_space=pltpu.VMEM)
    anywhere = pl.BlockSpec(memory_space=pl.ANY)
    wg, gg, gu, amax = pl.pallas_call(
        functools.partial(kernel, nz, ny),
        out_shape=(
            jax.ShapeDtypeStruct((dc, fh), BF16),
            jax.ShapeDtypeStruct((slots, fh), BF16),
            jax.ShapeDtypeStruct((slots, fh), BF16),
            jax.ShapeDtypeStruct((8, 128), F32),
        ),
        in_specs=[anywhere, vmem, vmem, anywhere, anywhere, anywhere],
        out_specs=(vmem,) * 4,
        scratch_shapes=scratch,
        compiler_params=pltpu.CompilerParams(
            collective_id=0, has_side_effects=True, vmem_limit_bytes=56 * 1024 * 1024
        ),
    )(out_grad, routing.T, route_probs.T, w_down[0], saved_gate, saved_up)
    return wg.reshape(w_down.shape), gg, gu, amax[0:1, 0:1]


def solution(mesh):
    placed = (
        P(("dp", "expert"), "tensor"),
        P(("dp", "expert"), None),
        P(("dp", "expert"), None),
        P("expert", "dp", "tensor"),
        P(("dp", "expert"), "tensor"),
        P(("dp", "expert"), "tensor"),
    )
    return jax.shard_map(
        functools.partial(body, math.isqrt(mesh.shape["expert"])),
        mesh=mesh,
        in_specs=placed,
        out_specs=(
            P("expert", "dp", "tensor"),
            P(("dp", "expert"), "tensor"),
            P(("dp", "expert"), "tensor"),
            P("dp", "expert"),
        ),
        check_vma=False,
    )
```

```python
import functools
import math

import jax
import jax.numpy as jnp
from jax import lax
from jax.experimental import pallas as pl
from jax.experimental.pallas import tpu as pltpu
from jax.sharding import PartitionSpec as P

MESH = pl.DeviceIdType.MESH
EPSILON = 1e-6
F32 = jnp.float32
BF16 = jnp.bfloat16


def kernel(
    nz, ny, og, ids, probs, w, gate, up,
    wg_out, gg_out, gu_out, amax_out,
    gv, uv, wv, a1, a2, tok, idb, prb, keyb, scb, S, X, act,
    gh, wacc, far_out, far_in, near_out, near_in, mx_out, mx_in,
    loc_sem, id_send, id_recv, pr_send, pr_recv, tok_send, tok_recv, tokf_send,
    act_send, act_recv, actf_send, actf_recv,
    a2a_send, a2a_recv, fwd_send, fwd_recv,
    far_send, far_recv, near_send, near_recv, mx_send, mx_recv,
):
    q = lax.axis_index("dp")
    e = lax.axis_index("expert")
    t = lax.axis_index("tensor")
    z = e // ny
    y = lax.rem(e, ny)
    half = nz // 2
    ne = nz * ny
    tokens, dc = tok.shape[1], tok.shape[2]
    top = ids.shape[0]
    cap = S.shape[3]
    lag = 3
    slots, fh = gate.shape
    sh = slots // 2
    right, opposite, left = lax.rem(q + 1, 4), lax.rem(q + 2, 4), lax.rem(q + 3, 4)
    partner = (q, e, 1 - t)

    def rcopy(src, dst, ss, rs, dev):
        return pltpu.make_async_remote_copy(
            src_ref=src, dst_ref=dst, send_sem=ss, recv_sem=rs, device_id=dev, device_id_type=MESH
        )

    copies = [
        pltpu.make_async_copy(source, target, loc_sem.at[n])
        for n, (source, target) in enumerate(((ids, idb.at[0]), (probs, prb.at[0]), (gate, gv), (up, uv), (w, wv)))
    ]
    for copy in copies:
        copy.start()

    barrier = pltpu.get_barrier_semaphore()

    def greet(n, carry):
        dz, dy = 2 * (n // ny) + t, lax.rem(n, ny)
        peer = lax.rem(z + dz, nz) * ny + lax.rem(y + dy, ny)

        @pl.when(dz + dy > 0)
        def _():
            pl.semaphore_signal(barrier, inc=1, device_id=(q, peer, t), device_id_type=MESH)

        return carry

    lax.fori_loop(0, half * ny, greet, 0)
    for r in range(1, 4):
        pl.semaphore_signal(barrier, inc=1, device_id=(lax.rem(q + r, 4), e, t), device_id_type=MESH)
    pl.semaphore_signal(barrier, inc=1, device_id=partner, device_id_type=MESH)

    rows = slots // nz

    def natural(n):
        return pl.ds(pl.multiple_of(lax.rem(z - n + nz, nz) * rows, rows), rows)

    def ordered(n):
        return pl.ds(pl.multiple_of(n * rows, rows), rows)

    def activate(n, carry):
        g = gv[natural(n), :].astype(F32)
        u = uv[natural(n), :].astype(F32)
        s = jax.nn.sigmoid(g)
        silu = g * s
        act[0, ordered(n), :] = (silu * u).astype(BF16)
        a1[ordered(n), :] = u * s * (1.0 + g * (1.0 - s))
        a2[ordered(n), :] = silu
        return carry

    copies[2].wait()
    copies[3].wait()
    lax.fori_loop(0, nz, activate, 0)

    def make_key(r):
        owner = lax.broadcasted_iota(jnp.int32, (ne, tokens), 0)
        routed = jnp.zeros((ne, tokens), F32)
        scale = jnp.zeros((ne, tokens), F32)
        for k in range(top):
            match = owner == idb[r, k : k + 1, :]
            routed = jnp.where(match, 1.0, routed)
            scale = scale + jnp.where(match, prb[r, k : k + 1, :], 0.0)
        before = lax.broadcasted_iota(jnp.int32, (tokens, tokens), 0)
        after = lax.broadcasted_iota(jnp.int32, (tokens, tokens), 1)
        upper = jnp.where(before < after, 1.0, 0.0).astype(BF16)
        rank = jnp.dot(routed.astype(BF16), upper, preferred_element_type=F32)
        keyb[r] = jnp.where(routed > 0.0, rank, -1.0)
        scb[r] = scale

    def token_chunk(n):
        j = lax.rem(q + n, 2)
        return 2 * t + j, og.at[:, pl.ds(pl.multiple_of(j * dc, 128), dc)]

    copies[0].wait()
    copies[1].wait()
    make_key(0)
    holder = lax.div(q, 2) == t

    @pl.when(holder)
    def _():
        pltpu.make_async_copy(token_chunk(0)[1], tok.at[0], tok_recv.at[0]).start()

    pl.semaphore_wait(barrier, half * ny + 3 + t)

    @pl.when(holder)
    def _():
        rcopy(token_chunk(0)[1], tok.at[0], tokf_send.at[0], tok_recv.at[0], partner).start()

    @pl.when(jnp.logical_not(holder))
    def _():
        dest, source = token_chunk(0)
        rcopy(source, tok.at[2], tok_send.at[0], tok_recv.at[2], (dest, e, t)).start()

    dest, source = token_chunk(1)
    slot = lax.rem(q - dest + 4, 4)
    rcopy(source, tok.at[slot], tok_send.at[1], tok_recv.at[slot], (dest, e, t)).start()
    for r in (2, 1, 3):
        peer = (lax.rem(q + r, 4), e, t)
        slot = (4 - r) % 4
        rcopy(ids, idb.at[slot], id_send.at[r], id_recv.at[slot], peer).start()
        rcopy(probs, prb.at[slot], pr_send.at[r], pr_recv.at[slot], peer).start()

    def get_tokens(r):
        if r > 0:
            rcopy(ids, idb.at[r], id_send.at[r], id_recv.at[r], partner).wait_recv()
            rcopy(probs, prb.at[r], pr_send.at[r], pr_recv.at[r], partner).wait_recv()
            make_key(r)
        rcopy(tok.at[r], tok.at[r], tokf_send.at[r], tok_recv.at[r], partner).wait_recv()
        if r > 0:

            @pl.when(holder)
            def _():
                rcopy(tok.at[r], tok.at[r], tokf_send.at[r], tok_recv.at[r], partner).start()

    rank_of = lax.broadcasted_iota(jnp.int32, (cap, tokens), 0).astype(F32)

    def build(r, i):
        zz = lax.rem(z + 2 * i + t, nz)
        at = pl.ds(pl.multiple_of(zz * ny, ny), ny)
        keys, scales = keyb[r, at, :], scb[r, at, :]
        picks, weights = [], []
        for yy in range(ny):
            hit = keys[yy : yy + 1, :] == rank_of
            picks.append(jnp.where(hit, 1.0, 0.0))
            weights.append(jnp.sum(jnp.where(hit, scales[yy : yy + 1, :], 0.0), axis=1, keepdims=True))
        pick = jnp.concatenate(picks, axis=0).astype(BF16)
        weight = jnp.concatenate(weights, axis=0)
        value = jnp.dot(pick, tok[r], preferred_element_type=F32) * weight
        for yy in range(ny):
            S[r, i, yy] = value[yy * cap : (yy + 1) * cap, :].astype(BF16)

    def send(r, i):
        dz = 2 * i + t
        zz = lax.rem(z + dz, nz)

        def one(k, carry):
            dy = lax.rem(jnp.where(lax.rem(k, 2) == 1, ny // 2 + (k + 1) // 2, ny // 2 - k // 2), ny)
            yy = lax.rem(y + dy, ny)
            row, target = S.at[r, i, yy], X.at[r, dz, y]

            @pl.when(dz + dy > 0)
            def _():
                rcopy(row, target, a2a_send.at[r, i], a2a_recv.at[r, i], (q, zz * ny + yy, t)).start()

            @pl.when(dz + dy == 0)
            def _():
                pltpu.make_async_copy(row, target, a2a_recv.at[r, i]).start()

            return carry

        lax.fori_loop(0, ny, one, 0)

    def arrive(r, i):
        block = X.at[r, 2 * i + t]
        rcopy(block, block, fwd_send.at[r, i], a2a_recv.at[r, i], partner).wait_recv()
        rcopy(block, block, fwd_send.at[r, i], fwd_recv.at[r, i], partner).start()

    def arrive_partner(r, i):
        block = X.at[r, 2 * i + 1 - t]
        rcopy(block, block, fwd_send.at[r, i], fwd_recv.at[r, i], partner).wait_recv()

    low, high = pl.ds(0, sh), pl.ds(sh, sh)
    parts = (low, high)

    def grad_hidden(r, h):
        block = X[r, h * half : (h + 1) * half].reshape(sh, dc)
        return jnp.dot(block, wv[...], preferred_element_type=F32)

    def weight_grad(r, init):
        step = 128

        def body(n, carry):
            at = pl.ds(pl.multiple_of(n * step, step), step)
            block = X[r, :, :, :, at].reshape(slots, step)
            value = lax.dot_general(block, act[r], (((0,), (0,)), ((), ())), preferred_element_type=F32)
            if init:
                wacc[at, :] = value
            else:
                wacc[at, :] += value
            return carry

        lax.fori_loop(0, dc // step, body, 0)

    def act_copy(n):
        dest, slot = ((right, 3), (left, 1))[n]
        return rcopy(act.at[0], act.at[slot], act_send.at[n], act_recv.at[n], (dest, e, t))

    def act_forward(n):
        dest, slot = ((right, 3), (left, 1))[n]
        return rcopy(act.at[slot, parts[n]], act.at[2, parts[n]], actf_send.at[n], actf_recv.at[n], (dest, e, t))

    def far_copy(n):
        dest = (right, left)[n]
        return rcopy(far_out.at[parts[n]], far_in.at[n], far_send.at[n], far_recv.at[n], (dest, e, t))

    def near_copy(n, h):
        dest = (right, left)[n]
        rows_h = parts[h]
        return rcopy(
            near_out.at[n, rows_h], near_in.at[n, rows_h], near_send.at[n, h], near_recv.at[n, h], (dest, e, t)
        )

    def hidden(r, h):
        value = grad_hidden(r, h)
        if r == 2:
            far_out[parts[h], :] = value.astype(BF16)
            far_copy(h).start()
        elif r == 0:
            gh[parts[h], :] = value
        else:
            n = 0 if r == 1 else 1
            if h == n:
                far_copy(n).wait_recv()
                value = value + far_in[n].astype(F32)
            near_out[n, parts[h], :] = value.astype(BF16)
            near_copy(n, h).start()

    last = max(1, half - 1)
    order = [(0, i) for i in range(last)]
    for r in (2, 1, 3):
        order += [(r, i) for i in range(half)]
    order += [(0, i) for i in range(last, half)]
    count = len(order)
    done = {}
    for k in range(count + lag + 1):
        if k < count:
            r, i = order[k]
            if i == 0:
                get_tokens(r)
            build(r, i)
            send(r, i)
        if k == last:
            act_copy(0).start()
            act_copy(1).start()
        if k == min(10, count):
            for n in range(2):
                act_copy(n).wait_recv()
                act_forward(n).start()
        if lag <= k < count + lag:
            arrive(*order[k - lag])
        if lag < k:
            r, i = order[k - lag - 1]
            arrive_partner(r, i)
            if k == lag + 1:
                copies[4].wait()
            if half == 1:
                hidden(r, 0)
                hidden(r, 1)
            elif i % (half // 2) == half // 2 - 1:
                hidden(r, i // (half // 2))
            if i == half - 1:
                if r == 1:
                    act_forward(0).wait_recv()
                    act_forward(1).wait_recv()
                    weight_grad(2, True)
                    weight_grad(1, False)
                elif r == 3:
                    weight_grad(3, False)
    assert order[-1][0] == 0 or half == 1
    for h in range(2):
        for n in range(2):
            near_copy(n, h).wait_recv()

    def total(n, largest):
        at = ordered(n)
        value = gh[at, :] + near_in[0, at, :].astype(F32) + near_in[1, at, :].astype(F32)
        gh[at, :] = value
        return jnp.maximum(largest, jnp.max(jnp.abs(value)))

    largest = lax.fori_loop(0, nz, total, jnp.zeros((), F32))
    mx_out[...] = jnp.full(mx_out.shape, largest, F32)
    exchange = rcopy(mx_out, mx_in, mx_send.at[0], mx_recv.at[0], partner)
    weight_grad(0, False)
    exchange.start()
    wg_out[...] = wacc[...].astype(BF16)
    exchange.wait_recv()
    amax = jnp.maximum(mx_out[...], mx_in[...])
    amax_out[...] = amax
    inverse = 1.0 / (amax[0:1, 0:1] + EPSILON)

    def scale_out(n, carry):
        at = ordered(n)
        quantized = (gh[at, :] * inverse).astype(BF16).astype(F32)
        gg_out[natural(n), :] = (quantized * a1[at, :]).astype(BF16)
        gu_out[natural(n), :] = (quantized * a2[at, :]).astype(BF16)
        return carry

    lax.fori_loop(0, nz, scale_out, 0)

    dest, source = token_chunk(1)
    rcopy(source, tok.at[0], tok_send.at[1], tok_recv.at[0], partner).wait_send()

    @pl.when(holder)
    def _():
        for r in range(4):
            rcopy(tok.at[r], tok.at[r], tokf_send.at[r], tok_recv.at[r], partner).wait_send()

    @pl.when(jnp.logical_not(holder))
    def _():
        rcopy(source, tok.at[0], tok_send.at[0], tok_recv.at[0], partner).wait_send()

    for r in range(1, 4):
        rcopy(ids, idb.at[r], id_send.at[r], id_recv.at[r], partner).wait_send()
        rcopy(probs, prb.at[r], pr_send.at[r], pr_recv.at[r], partner).wait_send()
    for n in range(2):
        act_copy(n).wait_send()
        act_forward(n).wait_send()
        far_copy(n).wait_send()
        for h in range(2):
            near_copy(n, h).wait_send()
    exchange.wait_send()
    for r in range(4):

        def drain(i, carry):
            block = X.at[r, 0]
            rcopy(block, block, fwd_send.at[r, i], fwd_recv.at[r, i], partner).wait_send()

            @pl.when(i + t > 0)
            def _():
                rcopy(S.at[r, 0], block, a2a_send.at[r, i], a2a_recv.at[r, i], partner).wait_send()

            @pl.when(i + t == 0)
            def _():
                some = pl.ds(0, ny - 1)
                rcopy(
                    S.at[r, 0, some], X.at[r, 0, some], a2a_send.at[r, i], a2a_recv.at[r, i], partner
                ).wait_send()

            return carry

        lax.fori_loop(0, half, drain, 0)


def body(side, out_grad, routing, route_probs, w_down, saved_gate, saved_up):
    nz = ny = side
    tokens, wide = out_grad.shape
    _, dc, fh = w_down.shape
    slots = saved_gate.shape[0]
    cap = slots // (nz * ny)
    top = routing.shape[1]
    half = nz // 2
    dma = pltpu.SemaphoreType.DMA
    scratch = [
        pltpu.VMEM((slots, fh), BF16),
        pltpu.VMEM((slots, fh), BF16),
        pltpu.VMEM((dc, fh), BF16),
        pltpu.VMEM((slots, fh), F32),
        pltpu.VMEM((slots, fh), F32),
        pltpu.VMEM((4, tokens, dc), BF16),
        pltpu.VMEM((4, top, tokens), jnp.int32),
        pltpu.VMEM((4, top, tokens), F32),
        pltpu.VMEM((4, nz * ny, tokens), F32),
        pltpu.VMEM((4, nz * ny, tokens), F32),
        pltpu.VMEM((4, half, ny, cap, dc), BF16),
        pltpu.VMEM((4, nz, ny, cap, dc), BF16),
        pltpu.VMEM((4, slots, fh), BF16),
        pltpu.VMEM((slots, fh), F32),
        pltpu.VMEM((dc, fh), F32),
        pltpu.VMEM((slots, fh), BF16),
        pltpu.VMEM((2, slots // 2, fh), BF16),
        pltpu.VMEM((2, slots, fh), BF16),
        pltpu.VMEM((2, slots, fh), BF16),
        pltpu.VMEM((8, 128), F32),
        pltpu.VMEM((8, 128), F32),
        dma((5,)),
        dma((4,)), dma((4,)), dma((4,)), dma((4,)),
        dma((2,)), dma((4,)), dma((4,)),
        dma((2,)), dma((2,)), dma((2,)), dma((2,)),
        dma((4, half)), dma((4, half)), dma((4, half)), dma((4, half)),
        dma((2,)), dma((2,)), dma((2, 2)), dma((2, 2)), dma((1,)), dma((1,)),
    ]
    vmem = pl.BlockSpec(memory_space=pltpu.VMEM)
    anywhere = pl.BlockSpec(memory_space=pl.ANY)
    wg, gg, gu, amax = pl.pallas_call(
        functools.partial(kernel, nz, ny),
        out_shape=(
            pltpu.VMEM((dc, fh), BF16),
            pltpu.VMEM((slots, fh), BF16),
            pltpu.VMEM((slots, fh), BF16),
            pltpu.VMEM((8, 128), F32),
        ),
        in_specs=[anywhere] * 6,
        out_specs=(vmem,) * 4,
        scratch_shapes=scratch,
        compiler_params=pltpu.CompilerParams(
            collective_id=0, has_side_effects=True, vmem_limit_bytes=65_000_000
        ),
    )(out_grad, routing.T, route_probs.T, w_down[0], saved_gate, saved_up)
    return wg.reshape(w_down.shape), gg, gu, amax[0:1, 0:1]


def solution(mesh):
    placed = (
        P(("dp", "expert"), "tensor"),
        P(("dp", "expert"), None),
        P(("dp", "expert"), None),
        P("expert", "dp", "tensor"),
        P(("dp", "expert"), "tensor"),
        P(("dp", "expert"), "tensor"),
    )
    return jax.shard_map(
        functools.partial(body, math.isqrt(mesh.shape["expert"])),
        mesh=mesh,
        in_specs=placed,
        out_specs=(
            P("expert", "dp", "tensor"),
            P(("dp", "expert"), "tensor"),
            P(("dp", "expert"), "tensor"),
            P("dp", "expert"),
        ),
        check_vma=False,
    )
```
